32 devices in a mesh: gx: 8 (over y, x, core), gz: 4 (over z).
Axes of the slice: x: 2, y: 2, z: 4, core: 2. Of those that a mesh axis runs over, the one named last changes fastest.
Arguments:
- pressure_now: float32 [128, 128, 512], P('gz', 'gx'), may hold values from -6 to 6
- pressure_prev: float32 [128, 128, 512], P('gz', 'gx'), may hold values from -6 to 6
- adjoint_now: float32 [128, 128, 512], P('gz', 'gx'), may hold values from -6 to 6
- adjoint_prev: float32 [128, 128, 512], P('gz', 'gx'), may hold values from -6 to 6
- speed2: float32 [128, 128, 512], P('gz', 'gx'), may hold values from 0.05 to 0.32
- layer_state: float32 [4096, 64, 128], P(('gx', 'gz')), may hold values from -3 to 3
- layer_maps: float32 [8, 64, 64], replicated, as said below
- send_rows: int32 [32, 32, 4], P(('gx', 'gz')), may hold values from -1 to 2047, as said below
- slot_patch: int32 [4096], P(('gx', 'gz')), may hold values from 0 to 255
- patch_material: int32 [256], replicated, may hold values from 0 to 7
Outputs:
- pressure_out: float32 [128, 128, 512], P('gz', 'gx')
- adjoint_out: float32 [128, 128, 512], P('gz', 'gx')
- patch_gradient: float32 [256, 128], P(('gx', 'gz'))
The draws below stay inside these ranges and needn't reach their ends.
Inputs may be any that keep to these rules, and one draw needn't show every extreme that they name: `send_rows`: each device's non-negative entries are distinct rows of its tile; -1 marks an unused entry; for one device every entry aimed at it is used. `layer_maps`: each material's matrix has diagonal entries from 0.5 to 0.9.
All inputs are finite; a program needn't handle non-finite values.
Results may differ from the reference program's by a relative error of at most 0.00016.
Values sent between devices are 32-bit elements; how exact they have to be, the bound alone decides.
A program may use at most 192 MiB of HBM per device.

```python
import math
import jax
import jax.numpy as jnp
import numpy as np
from jax import lax

CX = 16
CZ = 32
NY = 512
W = 128
DEPTH = 64
SLOT_DEV = 128
MATS = 8
STEPS = 4
NX = 128
NZ = 128
ROWS_TILE = 2048
CAP = 4
PATCHES = 256
N_GX = 8
N_GZ = 4
DEVICES = 32


def draw_layer_maps(key, part):
    first, second = jax.random.split(key)
    diag = jax.random.uniform(first, (MATS, DEPTH), jnp.float32, 0.5, 0.9)
    spread = 0.4 / math.sqrt(DEPTH)
    off = jax.random.normal(second, (MATS, DEPTH, DEPTH), jnp.float32) * spread
    ident = jnp.eye(DEPTH, dtype=jnp.float32)
    return ident[None, :, :] * diag[:, :, None] + off * (1.0 - ident[None, :, :])


def draw_send_rows(key, part):
    key_fill, key_full, key_coin, key_perm = jax.random.split(key, 4)
    fill = jax.random.randint(key_fill, (DEVICES,), 300, 1001)
    fullest = jax.random.randint(key_full, (), 0, DEVICES)
    fill = jnp.where(jnp.arange(DEVICES) == fullest, 1001, fill)
    coin = jax.random.randint(key_coin, (DEVICES, DEVICES, CAP), 0, 1000)
    live = coin < fill[None, :, None]
    keys = jax.random.split(key_perm, DEVICES)
    picks = jax.vmap(lambda single: jax.random.permutation(single, ROWS_TILE)[:SLOT_DEV])(keys)
    picks = picks.reshape(DEVICES, DEVICES, CAP).astype(jnp.int32)
    return jnp.where(live, picks, -1).astype(jnp.int32)


def set_ends(result, stream_key, low, top_value):
    spot = [jax.random.randint(jax.random.fold_in(stream_key, axis), (), 0, length) for axis, length in enumerate(result.shape)]
    widest = result.shape.index(max(result.shape))
    neighbour = spot[:widest] + [(spot[widest] + 1) % result.shape[widest]] + spot[widest + 1:]
    return result.at[tuple(spot)].set(low).at[tuple(neighbour)].set(top_value)


def block_levels(rng, dims, cuts, smallest, top_value):
    loudness = 1.0
    for dim, parts in cuts:
        draws = jax.random.uniform(jax.random.fold_in(jax.random.fold_in(rng, 6), dim), (parts,), jnp.float32, smallest / len(cuts), top_value / len(cuts))
        loudness = loudness * jnp.repeat(jnp.exp(draws), dims[dim] // parts).reshape((-1,) + (1,) * (len(dims) - 1 - dim))
    return loudness


def rank_bounds(amount, lean):
    loads = [(1 << 20) // math.isqrt(grade ** lean) + 1 for grade in range(1, amount + 1)]
    width = 1 + sum(loads) // (1 << 30)
    return np.cumsum(np.array([max(1, weight // width) for weight in loads]))


def skewed_ids(key, extent, count, skew):
    grid = rank_bounds(count, skew)
    lot = jax.random.randint(jax.random.fold_in(key, 1), extent, 0, int(grid[count - 1]))
    rank = jnp.searchsorted(jnp.asarray(grid, jnp.int32), lot, side="right")
    return jax.random.permutation(jax.random.fold_in(key, 2), count)[rank].astype(jnp.int32)


def normal_values(rng, dims, deviation, reach, cuts=(), kind=jnp.bfloat16):
    entries = jax.random.normal(rng, dims, jnp.float32) * deviation
    if len(cuts) > 0:
        entries = block_levels(rng, dims, cuts, -0.22, 0.18) * entries
    return jnp.clip(entries, min=-reach, max=reach).astype(kind)


def setup_inputs(seed: int = 0) -> dict:
    seeds = jax.random.split(jax.random.key(seed), 11)
    pressure_now = normal_values(seeds[0], (NZ, NX, NY), 1.0, 6.0, ((0, 4), (1, 8)), jnp.float32)
    pressure_prev = normal_values(seeds[1], (NZ, NX, NY), 1.0, 6.0, ((0, 4), (1, 8)), jnp.float32)
    adjoint_now = normal_values(seeds[2], (NZ, NX, NY), 1.0, 6.0, ((0, 4), (1, 8)), jnp.float32)
    adjoint_prev = normal_values(seeds[3], (NZ, NX, NY), 1.0, 6.0, ((0, 4), (1, 8)), jnp.float32)
    speed2 = jnp.clip(jnp.exp(math.log(0.32) - 1.856298 * jax.random.uniform(seeds[4], (NZ, NX, NY), jnp.float32) ** block_levels(seeds[4], (NZ, NX, NY), ((0, 4), (1, 8)), -0.2, 0.2)), 0.05, 0.32)
    layer_state = normal_values(seeds[5], (DEVICES * SLOT_DEV, DEPTH, W), 0.5, 3.0, ((0, 32),), jnp.float32)
    layer_maps = draw_layer_maps(jax.random.fold_in(seeds[10], 71), 0)
    send_rows = draw_send_rows(jax.random.fold_in(seeds[10], 71), 0)
    slot_patch = set_ends(skewed_ids(seeds[8], (DEVICES * SLOT_DEV,), PATCHES, 2), jax.random.fold_in(seeds[8], 3), 0, PATCHES - 1).astype(jnp.int32)
    patch_material = set_ends(jax.random.randint(seeds[9], (PATCHES,), 0, MATS), jax.random.fold_in(seeds[9], 1), 0, MATS - 1).astype(jnp.int32)
    return dict(pressure_now=pressure_now, pressure_prev=pressure_prev, adjoint_now=adjoint_now, adjoint_prev=adjoint_prev, speed2=speed2, layer_state=layer_state, layer_maps=layer_maps, send_rows=send_rows, slot_patch=slot_patch, patch_material=patch_material)


KAPPA = 0.5
BETA = 0.3


def to_rows(field):
    blocks = field.reshape(N_GZ, CZ, N_GX, CX, NY // W, W).transpose(2, 0, 1, 3, 4, 5)
    return blocks.reshape(N_GX * N_GZ, CZ * CX * (NY // W), W)


def from_rows(rows):
    blocks = rows.reshape(N_GX, N_GZ, CZ, CX, NY // W, W).transpose(1, 2, 0, 3, 4, 5)
    return blocks.reshape(N_GZ * CZ, N_GX * CX, NY)


def laplace(field):
    padded = jnp.pad(field, 1)
    beside = padded[2:, 1:-1, 1:-1] + padded[:-2, 1:-1, 1:-1]
    beside = beside + padded[1:-1, 2:, 1:-1] + padded[1:-1, :-2, 1:-1]
    beside = beside + padded[1:-1, 1:-1, 2:] + padded[1:-1, 1:-1, :-2]
    return beside - 6.0 * field


def place_rows(target, delta):
    empty = jnp.zeros((ROWS_TILE, W), jnp.float32)
    return empty.at[target].add(delta, mode="drop")


def relay_step(field, previous, speed2, layer, maps, send_rows):
    devices = N_GX * N_GZ
    rows = to_rows(field)
    sources = send_rows.reshape(devices, SLOT_DEV)
    valid = sources >= 0
    picked = jnp.take_along_axis(rows, jnp.maximum(sources, 0)[:, :, None], axis=1)
    picked = jnp.where(valid[:, :, None], picked, 0.0)
    air = picked.reshape(devices, devices, CAP, W).transpose(1, 0, 2, 3).reshape(devices * SLOT_DEV, W)
    push = KAPPA * (air - layer[:, 0, :])
    fresh = jnp.einsum("sij,sjw->siw", maps, layer, precision=lax.Precision.HIGHEST)
    fresh = fresh + maps[:, :, 0][:, :, None] * push[:, None, :]
    back = fresh[:, 0, :].reshape(devices, devices, CAP, W).transpose(1, 0, 2, 3).reshape(devices, SLOT_DEV, W)
    delta = jnp.where(valid[:, :, None], BETA * (back - picked), 0.0)
    target = jnp.where(valid, sources, ROWS_TILE).astype(jnp.int32)
    coupling = jax.vmap(place_rows)(target, delta)
    following = 2.0 * field - previous + speed2 * laplace(field) + from_rows(coupling)
    return following, fresh


def reference(pressure_now, pressure_prev, adjoint_now, adjoint_prev, speed2, layer_state, layer_maps, send_rows, slot_patch, patch_material):
    materials = jnp.take(patch_material, slot_patch)
    forward_maps = jnp.take(layer_maps, materials, axis=0)
    adjoint_maps = jnp.swapaxes(forward_maps, 1, 2)
    layer_f = layer_state
    layer_a = jnp.zeros_like(layer_state)
    forward_layers = []
    adjoint_layers = []
    for step in range(STEPS):
        following, layer_f = relay_step(pressure_now, pressure_prev, speed2, layer_f, forward_maps, send_rows)
        pressure_prev, pressure_now = pressure_now, following
        following, layer_a = relay_step(adjoint_now, adjoint_prev, speed2, layer_a, adjoint_maps, send_rows)
        adjoint_prev, adjoint_now = adjoint_now, following
        forward_layers.append(layer_f)
        adjoint_layers.append(layer_a)
    correlation = jnp.zeros((layer_state.shape[0], W), jnp.float32)
    for step in range(STEPS):
        correlation = correlation + jnp.sum(forward_layers[step] * adjoint_layers[STEPS - 1 - step], axis=1)
    patch_gradient = jax.ops.segment_sum(correlation, slot_patch, num_segments=PATCHES)
    return pressure_now, adjoint_now, patch_gradient
```

```python
import functools

import jax
import jax.numpy as jnp
from jax import lax
from jax.experimental import pallas as pl
from jax.experimental.pallas import tpu as pltpu
from jax.sharding import PartitionSpec as P

STEPS = 4
KAPPA = 0.5
BETA = 0.3
ROWS = 2 * STEPS + 1
LANES = 128


def project_kernel(block, slot_patch, patch_material, maps, state, out, table, info):
    mats, depth, _ = maps.shape
    lane = lax.broadcasted_iota(jnp.int32, (1, depth), 1)
    halve = jnp.where(lane == 0, 1.0 - KAPPA, 1.0)
    row8 = lax.broadcasted_iota(jnp.int32, (8, LANES), 0)
    lane8 = lax.broadcasted_iota(jnp.int32, (8, LANES), 1)

    @pl.when(pl.program_id(0) == 0)
    def _():
        @pl.loop(0, mats)
        def _(m):
            full = maps[m]
            v = full[0:1, :]
            h = jnp.zeros_like(v)
            surface, inner = [], []
            for n in range(STEPS):
                dv = v * halve
                surface.append(dv)
                pair = jnp.concatenate([dv, v + h] + [jnp.zeros_like(v)] * 6, axis=0)
                got = jnp.dot(
                    pair, full, precision=lax.Precision.HIGHEST,
                    preferred_element_type=jnp.float32,
                )
                v = got[0:1]
                h = got[1:2] * halve
                inner.append(h)
            rows = jnp.concatenate(surface + inner, axis=0)
            table[m] = rows
            first = rows[:, 0:1] / (1.0 - KAPPA)
            info[m] = jnp.sum(jnp.where(row8 == lane8, first, 0.0), axis=0, keepdims=True)

    base = pl.program_id(0) * block
    lane1 = lax.broadcasted_iota(jnp.int32, (1, LANES), 1)

    for i in range(block):
        patch = slot_patch[base + i]
        mat = patch_material[patch]
        got = jnp.dot(
            table[mat], state[i], precision=lax.Precision.HIGHEST,
            preferred_element_type=jnp.float32,
        )
        for n in range(2 * STEPS):
            out[n, i : i + 1, :] = got[n : n + 1]
        patches = jnp.full((1, LANES), patch, jnp.int32).astype(jnp.float32)
        out[2 * STEPS, i : i + 1, :] = jnp.where(lane1 == ROWS - 1, patches, info[mat])


def project(slot_patch, patch_material, maps, state):
    slots, depth, width = state.shape
    mats = maps.shape[0]
    block = 16
    return pl.pallas_call(
        functools.partial(project_kernel, block),
        out_shape=jax.ShapeDtypeStruct((ROWS, slots, width), jnp.float32),
        grid_spec=pltpu.PrefetchScalarGridSpec(
            num_scalar_prefetch=2,
            grid=(slots // block,),
            in_specs=[
                pl.BlockSpec((mats, depth, depth), lambda i, *_: (0, 0, 0)),
                pl.BlockSpec((block, depth, width), lambda i, *_: (i, 0, 0)),
            ],
            out_specs=pl.BlockSpec((ROWS, block, width), lambda i, *_: (0, i, 0)),
            scratch_shapes=[
                pltpu.VMEM((mats, 2 * STEPS, depth), jnp.float32),
                pltpu.VMEM((mats, 1, width), jnp.float32),
            ],
        ),
    )(slot_patch, patch_material, maps, state)


def wave_kernel(
    nx, nz,
    p_now, p_prev, a_now, a_prev, speed2, src_lane, src_column, relay,
    p_out, a_out, corr,
    p_mid, a_mid, spread, pick, couple, hist,
    x_send, x_recv, z_recv, send_sem, recv_sem,
):
    cz, cx, ny = speed2.shape
    slots = relay.shape[1]
    blocks = ny // LANES
    gx, gz = lax.axis_index("gx"), lax.axis_index("gz")
    exists = [gx > 0, gx < nx - 1, gz > 0, gz < nz - 1]
    target = [(gx - 1, gz), (gx + 1, gz), (gx, gz - 1), (gx, gz + 1)]

    barrier = pltpu.get_barrier_semaphore()
    for d in range(4):
        @pl.when(exists[d])
        def _(d=d):
            pl.semaphore_signal(
                barrier, inc=1, device_id=target[d], device_id_type=pl.DeviceIdType.MESH
            )
    pl.semaphore_wait(barrier, sum(peer.astype(jnp.int32) for peer in exists))

    now = (p_now, a_now)
    prev = (p_prev, a_prev)
    mid = (p_mid, a_mid)
    outs = (p_out, a_out)

    def halo_copy(field, step, d, source):
        if d < 2:
            ref, dst = x_send.at[step, field, d], x_recv.at[step, field, 1 - d]
        else:
            ref = source.at[0 if d == 2 else cz - 1]
            dst = z_recv.at[step, field, 3 - d]
        return pltpu.make_async_remote_copy(
            src_ref=ref, dst_ref=dst,
            send_sem=send_sem.at[step, field, d],
            recv_sem=recv_sem.at[step, field, d ^ 1],
            device_id=target[d], device_id_type=pl.DeviceIdType.MESH,
        )

    def start_halo(field, step, source):
        for d in range(4):
            @pl.when(exists[d])
            def _(d=d):
                halo_copy(field, step, d, source).start()

    def wait_recv(field, step, source):
        for d in range(4):
            @pl.when(exists[d])
            def _(d=d):
                side = x_recv.at[step, field, d] if d < 2 else z_recv.at[step, field, d - 2]
                pltpu.make_async_remote_copy(
                    src_ref=side, dst_ref=side,
                    send_sem=send_sem.at[step, field, d],
                    recv_sem=recv_sem.at[step, field, d],
                    device_id=target[d], device_id_type=pl.DeviceIdType.MESH,
                ).wait_recv()

    def wait_send(field, step, source):
        for d in range(4):
            @pl.when(exists[d])
            def _(d=d):
                halo_copy(field, step, d, source).wait_send()

    for field in range(2):
        @pl.loop(0, cz)
        def _(z, field=field):
            x_send[0, field, 0, pl.ds(z, 1), :] = now[field][z, 0:1, :]
            x_send[0, field, 1, pl.ds(z, 1), :] = now[field][z, cx - 1 : cx, :]
        start_halo(field, 0, now[field])

    for d in range(4):
        @pl.when(jnp.logical_not(exists[d]))
        def _(d=d):
            for step in range(STEPS):
                for field in range(2):
                    if d < 2:
                        x_recv[step, field, d] = jnp.zeros((cz, ny), jnp.float32)
                    else:
                        z_recv[step, field, d - 2] = jnp.zeros((cx, ny), jnp.float32)

    lanes = src_lane[...]
    xrow = lax.broadcasted_iota(jnp.int32, (cx, slots), 0)

    @pl.loop(0, cz)
    def _(z):
        for rb in range(blocks):
            row = z * (cx * blocks) + xrow * blocks + rb
            hit = jnp.where(row == lanes, 1.0, 0.0).astype(jnp.bfloat16)
            spread[rb, pl.ds(pl.multiple_of(z * cx, cx), cx), :] = jnp.concatenate([hit, hit], axis=1)

    lane_row = lax.broadcasted_iota(jnp.int32, (slots, cz * cx), 1) * blocks
    column = src_column[...]
    for rb in range(blocks):
        pick[rb] = jnp.where(lane_row + rb == column, 1.0, 0.0).astype(jnp.bfloat16)

    def gather(source, field, step):
        picked = jnp.zeros((slots, LANES), jnp.float32)
        for rb in range(blocks):
            value = source[:, :, rb * LANES : (rb + 1) * LANES].reshape(cz * cx, LANES)
            high = value.astype(jnp.bfloat16)
            low = (value - high.astype(jnp.float32)).astype(jnp.bfloat16)
            for part in (high, low):
                picked = picked + jnp.dot(pick[rb], part, preferred_element_type=jnp.float32)
        hist[field, step] = picked

    def coef(n):
        return relay[ROWS - 1, :, n : n + 1]

    row_id = lax.broadcasted_iota(jnp.int32, (cx, ny), 0)
    lane_id = lax.broadcasted_iota(jnp.int32, (cx, ny), 1)

    for step in range(STEPS):
        for field in range(2):
            current = (now, mid, outs, mid)[step][field]
            earlier = (prev, now, mid, outs)[step][field]
            result = (mid, outs, mid, outs)[step][field]
            last = step == STEPS - 1

            gather(current, field, step)
            back = relay[step] if field == 0 else jnp.zeros((slots, LANES), jnp.float32)
            for t in range(step + 1):
                back = back + KAPPA * coef(step - t) * hist[field, t]
            delta = BETA * (back - hist[field, step])
            high = delta.astype(jnp.bfloat16)
            low = (delta - high.astype(jnp.float32)).astype(jnp.bfloat16)
            both = jnp.concatenate([high, low], axis=0)

            @pl.loop(0, blocks)
            def _(rb):
                couple[rb] = jnp.dot(spread[rb], both, preferred_element_type=jnp.float32)

            wait_recv(field, step, current)
            if step > 0:
                wait_send(field, step - 1, earlier)

            def plane(z, down, up):
                f = current[z]
                at = pl.multiple_of(z * cx, cx) if not isinstance(z, int) else z * cx
                lo = x_recv[step, field, 0, pl.ds(z, 1), :]
                hi = x_recv[step, field, 1, pl.ds(z, 1), :]
                west = jnp.where(row_id == 0, lo, pltpu.roll(f, 1, 0))
                east = jnp.where(row_id == cx - 1, hi, pltpu.roll(f, cx - 1, 0))
                south = jnp.where(lane_id == 0, 0.0, pltpu.roll(f, 1, 1))
                north = jnp.where(lane_id == ny - 1, 0.0, pltpu.roll(f, ny - 1, 1))
                beside = (down + up) + (west + east) + (south + north)
                extra = jnp.concatenate([couple[rb, pl.ds(at, cx), :] for rb in range(blocks)], axis=1)
                new = 2.0 * f - earlier[z] + speed2[z] * (beside - 6.0 * f) + extra
                result[z] = new
                if not last:
                    x_send[step + 1, field, 0, pl.ds(z, 1), :] = new[0:1]
                    x_send[step + 1, field, 1, pl.ds(z, 1), :] = new[cx - 1 : cx]

            plane(0, z_recv[step, field, 0], current[1])
            plane(cz - 1, current[cz - 2], z_recv[step, field, 1])

            @pl.loop(1, cz - 1)
            def _(z):
                plane(z, current[z - 1], current[z + 1])

            if last:
                wait_send(field, step, current)
            else:
                start_halo(field, step + 1, result)

    total = jnp.zeros((slots, LANES), jnp.float32)
    for t in range(STEPS):
        inner = relay[2 * STEPS - 1 - t]
        for other in range(STEPS - t):
            inner = inner + KAPPA * coef(STEPS + STEPS - 1 - t - other) * hist[0, other]
        total = total + KAPPA * hist[1, t] * inner
    corr[...] = total


def wave(nx, nz, p_now, p_prev, a_now, a_prev, speed2, src, relay):
    cz, cx, ny = speed2.shape
    slots = relay.shape[1]
    f32 = jnp.float32
    vmem = pl.BlockSpec(memory_space=pltpu.VMEM)
    return pl.pallas_call(
        functools.partial(wave_kernel, nx, nz),
        out_shape=(
            jax.ShapeDtypeStruct((cz, cx, ny), f32),
            jax.ShapeDtypeStruct((cz, cx, ny), f32),
            jax.ShapeDtypeStruct((slots, LANES), f32),
        ),
        in_specs=[vmem] * 8,
        out_specs=(vmem, vmem, vmem),
        scratch_shapes=[
            pltpu.VMEM((cz, cx, ny), f32),
            pltpu.VMEM((cz, cx, ny), f32),
            pltpu.VMEM((ny // LANES, cz * cx, 2 * slots), jnp.bfloat16),
            pltpu.VMEM((ny // LANES, slots, cz * cx), jnp.bfloat16),
            pltpu.VMEM((ny // LANES, cz * cx, LANES), f32),
            pltpu.VMEM((2, STEPS, slots, LANES), f32),
            pltpu.VMEM((STEPS, 2, 2, cz, ny), f32),
            pltpu.VMEM((STEPS, 2, 2, cz, ny), f32),
            pltpu.VMEM((STEPS, 2, 2, cx, ny), f32),
            pltpu.SemaphoreType.DMA((STEPS, 2, 4)),
            pltpu.SemaphoreType.DMA((STEPS, 2, 4)),
        ],
        compiler_params=pltpu.CompilerParams(
            collective_id=0, has_side_effects=True, vmem_limit_bytes=50 * 1024 * 1024
        ),
    )(p_now, p_prev, a_now, a_prev, speed2, src.reshape(1, slots), src.reshape(slots, 1), relay)


def body(
    nx, nz, pressure_now, pressure_prev, adjoint_now, adjoint_prev, speed2,
    layer_state, layer_maps, send_rows, slot_patch, patch_material,
):
    slots, _, width = layer_state.shape
    devices = nx * nz
    patches = patch_material.shape[0]
    cap = send_rows.shape[2]
    axes = ("gx", "gz")
    rows = project(slot_patch, patch_material, layer_maps, layer_state)
    relay = lax.all_to_all(
        rows.reshape(ROWS, devices, cap, width), axes, split_axis=1, concat_axis=1, tiled=True
    ).reshape(ROWS, slots, width)
    pressure_out, adjoint_out, corr = wave(
        nx, nz, pressure_now, pressure_prev, adjoint_now, adjoint_prev, speed2,
        send_rows.reshape(-1), relay,
    )
    patch = relay[ROWS - 1, :, ROWS - 1].astype(jnp.int32)
    owners = (patch[:, None] == jnp.arange(patches, dtype=jnp.int32)[None, :]).astype(jnp.float32)
    local = jnp.einsum("sp,sw->pw", owners, corr, precision=lax.Precision.HIGHEST)
    gradient = lax.psum_scatter(local, axes, scatter_dimension=0, tiled=True)
    return pressure_out, adjoint_out, gradient


def solution(mesh):
    in_specs = (
        P("gz", "gx", None),
        P("gz", "gx", None),
        P("gz", "gx", None),
        P("gz", "gx", None),
        P("gz", "gx", None),
        P(("gx", "gz"), None, None),
        P(),
        P(("gx", "gz"), None, None),
        P(("gx", "gz")),
        P(),
    )
    out_specs = (P("gz", "gx", None), P("gz", "gx", None), P(("gx", "gz"), None))
    return jax.shard_map(
        functools.partial(body, mesh.shape["gx"], mesh.shape["gz"]),
        mesh=mesh, in_specs=in_specs, out_specs=out_specs, check_vma=False,
    )
```

```python
import functools

import jax
import jax.numpy as jnp
from jax import lax
from jax.experimental import pallas as pl
from jax.experimental.pallas import tpu as pltpu
from jax.sharding import PartitionSpec as P

STEPS = 4
KAPPA = 0.5
BETA = 0.3
ROWS = 2 * STEPS + 1
LANES = 128


def project_kernel(block, slot_patch, patch_material, maps, state, out, table, info):
    mats, depth, _ = maps.shape
    lane = lax.broadcasted_iota(jnp.int32, (1, depth), 1)
    halve = jnp.where(lane == 0, 1.0 - KAPPA, 1.0)
    row8 = lax.broadcasted_iota(jnp.int32, (8, LANES), 0)
    lane8 = lax.broadcasted_iota(jnp.int32, (8, LANES), 1)

    @pl.when(pl.program_id(0) == 0)
    def _():
        @pl.loop(0, mats)
        def _(m):
            full = maps[m]
            v = full[0:1, :]
            h = jnp.zeros_like(v)
            surface, inner = [], []
            for n in range(STEPS):
                dv = v * halve
                surface.append(dv)
                pair = jnp.concatenate([dv, v + h] + [jnp.zeros_like(v)] * 6, axis=0)
                got = jnp.dot(
                    pair, full, precision=lax.Precision.HIGHEST,
                    preferred_element_type=jnp.float32,
                )
                v = got[0:1]
                h = got[1:2] * halve
                inner.append(h)
            rows = jnp.concatenate(surface + inner, axis=0)
            high = rows.astype(jnp.bfloat16)
            low = (rows - high.astype(jnp.float32)).astype(jnp.bfloat16)
            table[m] = jnp.concatenate(
                [
                    jnp.concatenate([high, high], axis=1),
                    jnp.concatenate([low, jnp.zeros_like(low)], axis=1),
                ],
                axis=0,
            )
            first = rows[:, 0:1] / (1.0 - KAPPA)
            info[m] = jnp.sum(jnp.where(row8 == lane8, first, 0.0), axis=0, keepdims=True)

    base = pl.program_id(0) * block
    lane1 = lax.broadcasted_iota(jnp.int32, (1, LANES), 1)

    for i in range(block):
        patch = slot_patch[base + i]
        mat = patch_material[patch]
        start = state[i]
        high = start.astype(jnp.bfloat16)
        low = (start - high.astype(jnp.float32)).astype(jnp.bfloat16)
        both = jnp.dot(
            table[mat], jnp.concatenate([high, low], axis=0), preferred_element_type=jnp.float32
        )
        got = both[: 2 * STEPS] + both[2 * STEPS :]
        for n in range(2 * STEPS):
            out[n, i : i + 1, :] = got[n : n + 1]
        patches = jnp.full((1, LANES), patch, jnp.int32).astype(jnp.float32)
        out[2 * STEPS, i : i + 1, :] = jnp.where(lane1 == ROWS - 1, patches, info[mat])


def project(slot_patch, patch_material, maps, state):
    slots, depth, width = state.shape
    mats = maps.shape[0]
    block = 16
    return pl.pallas_call(
        functools.partial(project_kernel, block),
        out_shape=jax.ShapeDtypeStruct((ROWS, slots, width), jnp.float32),
        grid_spec=pltpu.PrefetchScalarGridSpec(
            num_scalar_prefetch=2,
            grid=(slots // block,),
            in_specs=[
                pl.BlockSpec((mats, depth, depth), lambda i, *_: (0, 0, 0)),
                pl.BlockSpec((block, depth, width), lambda i, *_: (i, 0, 0)),
            ],
            out_specs=pl.BlockSpec((ROWS, block, width), lambda i, *_: (0, i, 0)),
            scratch_shapes=[
                pltpu.VMEM((mats, 4 * STEPS, 2 * depth), jnp.bfloat16),
                pltpu.VMEM((mats, 1, width), jnp.float32),
            ],
        ),
    )(slot_patch, patch_material, maps, state)


def wave_kernel(
    nx, nz,
    p_now, p_prev, a_now, a_prev, speed2, src_lane, src_column, relay,
    p_out, a_out, corr,
    p_mid, a_mid, spread, pick, couple, hist,
    x_send, x_recv, z_recv, send_sem, recv_sem,
):
    cz, cx, ny = speed2.shape
    slots = relay.shape[1]
    blocks = ny // LANES
    gx, gz = lax.axis_index("gx"), lax.axis_index("gz")
    exists = [gx > 0, gx < nx - 1, gz > 0, gz < nz - 1]
    target = [(gx - 1, gz), (gx + 1, gz), (gx, gz - 1), (gx, gz + 1)]

    barrier = pltpu.get_barrier_semaphore()
    for d in range(4):
        @pl.when(exists[d])
        def _(d=d):
            pl.semaphore_signal(
                barrier, inc=1, device_id=target[d], device_id_type=pl.DeviceIdType.MESH
            )
    pl.semaphore_wait(barrier, sum(peer.astype(jnp.int32) for peer in exists))

    now = (p_now, a_now)
    prev = (p_prev, a_prev)
    mid = (p_mid, a_mid)
    outs = (p_out, a_out)

    def halo_copy(field, step, d, source):
        if d < 2:
            ref, dst = x_send.at[step, field, d], x_recv.at[step, field, 1 - d]
        else:
            ref = source.at[0 if d == 2 else cz - 1]
            dst = z_recv.at[step, field, 3 - d]
        return pltpu.make_async_remote_copy(
            src_ref=ref, dst_ref=dst,
            send_sem=send_sem.at[step, field, d],
            recv_sem=recv_sem.at[step, field, d ^ 1],
            device_id=target[d], device_id_type=pl.DeviceIdType.MESH,
        )

    def start_halo(field, step, source):
        for d in range(4):
            @pl.when(exists[d])
            def _(d=d):
                halo_copy(field, step, d, source).start()

    def wait_recv(field, step, source):
        for d in range(4):
            @pl.when(exists[d])
            def _(d=d):
                side = x_recv.at[step, field, d] if d < 2 else z_recv.at[step, field, d - 2]
                pltpu.make_async_remote_copy(
                    src_ref=side, dst_ref=side,
                    send_sem=send_sem.at[step, field, d],
                    recv_sem=recv_sem.at[step, field, d],
                    device_id=target[d], device_id_type=pl.DeviceIdType.MESH,
                ).wait_recv()

    def wait_send(field, step, source):
        for d in range(4):
            @pl.when(exists[d])
            def _(d=d):
                halo_copy(field, step, d, source).wait_send()

    for field in range(2):
        @pl.loop(0, cz)
        def _(z, field=field):
            x_send[0, field, 0, pl.ds(z, 1), :] = now[field][z, 0:1, :]
            x_send[0, field, 1, pl.ds(z, 1), :] = now[field][z, cx - 1 : cx, :]
        start_halo(field, 0, now[field])

    for d in range(4):
        @pl.when(jnp.logical_not(exists[d]))
        def _(d=d):
            for step in range(STEPS):
                for field in range(2):
                    if d < 2:
                        x_recv[step, field, d] = jnp.zeros((cz, ny), jnp.float32)
                    else:
                        z_recv[step, field, d - 2] = jnp.zeros((cx, ny), jnp.float32)

    lanes = src_lane[...]
    xrow = lax.broadcasted_iota(jnp.int32, (cx, slots), 0)

    @pl.loop(0, cz)
    def _(z):
        for rb in range(blocks):
            row = z * (cx * blocks) + xrow * blocks + rb
            hit = jnp.where(row == lanes, 1.0, 0.0).astype(jnp.bfloat16)
            spread[rb, pl.ds(pl.multiple_of(z * cx, cx), cx), :] = jnp.concatenate([hit, hit], axis=1)

    lane_row = lax.broadcasted_iota(jnp.int32, (slots, cz * cx), 1) * blocks
    column = src_column[...]
    for rb in range(blocks):
        pick[rb] = jnp.where(lane_row + rb == column, 1.0, 0.0).astype(jnp.bfloat16)

    def gather(source, field, step):
        picked = jnp.zeros((slots, LANES), jnp.float32)
        for rb in range(blocks):
            value = source[:, :, rb * LANES : (rb + 1) * LANES].reshape(cz * cx, LANES)
            high = value.astype(jnp.bfloat16)
            low = (value - high.astype(jnp.float32)).astype(jnp.bfloat16)
            for part in (high, low):
                picked = picked + jnp.dot(pick[rb], part, preferred_element_type=jnp.float32)
        hist[field, step] = picked

    def coef(n):
        return relay[ROWS - 1, :, n : n + 1]

    row_id = lax.broadcasted_iota(jnp.int32, (cx, ny), 0)
    lane_id = lax.broadcasted_iota(jnp.int32, (cx, ny), 1)

    for step in range(STEPS):
        for field in range(2):
            current = (now, mid, outs, mid)[step][field]
            earlier = (prev, now, mid, outs)[step][field]
            result = (mid, outs, mid, outs)[step][field]
            last = step == STEPS - 1

            gather(current, field, step)
            back = relay[step] if field == 0 else jnp.zeros((slots, LANES), jnp.float32)
            for t in range(step + 1):
                back = back + KAPPA * coef(step - t) * hist[field, t]
            delta = BETA * (back - hist[field, step])
            high = delta.astype(jnp.bfloat16)
            low = (delta - high.astype(jnp.float32)).astype(jnp.bfloat16)
            both = jnp.concatenate([high, low], axis=0)

            @pl.loop(0, blocks)
            def _(rb):
                couple[rb] = jnp.dot(spread[rb], both, preferred_element_type=jnp.float32)

            wait_recv(field, step, current)
            if step > 0:
                wait_send(field, step - 1, earlier)

            def plane(z, down, up):
                f = current[z]
                at = pl.multiple_of(z * cx, cx) if not isinstance(z, int) else z * cx
                lo = x_recv[step, field, 0, pl.ds(z, 1), :]
                hi = x_recv[step, field, 1, pl.ds(z, 1), :]
                west = jnp.where(row_id == 0, lo, pltpu.roll(f, 1, 0))
                east = jnp.where(row_id == cx - 1, hi, pltpu.roll(f, cx - 1, 0))
                south = jnp.where(lane_id == 0, 0.0, pltpu.roll(f, 1, 1))
                north = jnp.where(lane_id == ny - 1, 0.0, pltpu.roll(f, ny - 1, 1))
                beside = (down + up) + (west + east) + (south + north)
                extra = jnp.concatenate([couple[rb, pl.ds(at, cx), :] for rb in range(blocks)], axis=1)
                new = 2.0 * f - earlier[z] + speed2[z] * (beside - 6.0 * f) + extra
                result[z] = new
                if not last:
                    x_send[step + 1, field, 0, pl.ds(z, 1), :] = new[0:1]
                    x_send[step + 1, field, 1, pl.ds(z, 1), :] = new[cx - 1 : cx]

            plane(0, z_recv[step, field, 0], current[1])
            plane(cz - 1, current[cz - 2], z_recv[step, field, 1])

            @pl.loop(1, cz - 1)
            def _(z):
                plane(z, current[z - 1], current[z + 1])

            if last:
                wait_send(field, step, current)
            else:
                start_halo(field, step + 1, result)

    total = jnp.zeros((slots, LANES), jnp.float32)
    for t in range(STEPS):
        inner = relay[2 * STEPS - 1 - t]
        for other in range(STEPS - t):
            inner = inner + KAPPA * coef(STEPS + STEPS - 1 - t - other) * hist[0, other]
        total = total + KAPPA * hist[1, t] * inner
    corr[...] = total


def wave(nx, nz, p_now, p_prev, a_now, a_prev, speed2, src, relay):
    cz, cx, ny = speed2.shape
    slots = relay.shape[1]
    f32 = jnp.float32
    vmem = pl.BlockSpec(memory_space=pltpu.VMEM)
    return pl.pallas_call(
        functools.partial(wave_kernel, nx, nz),
        out_shape=(
            jax.ShapeDtypeStruct((cz, cx, ny), f32),
            jax.ShapeDtypeStruct((cz, cx, ny), f32),
            jax.ShapeDtypeStruct((slots, LANES), f32),
        ),
        in_specs=[vmem] * 8,
        out_specs=(vmem, vmem, vmem),
        scratch_shapes=[
            pltpu.VMEM((cz, cx, ny), f32),
            pltpu.VMEM((cz, cx, ny), f32),
            pltpu.VMEM((ny // LANES, cz * cx, 2 * slots), jnp.bfloat16),
            pltpu.VMEM((ny // LANES, slots, cz * cx), jnp.bfloat16),
            pltpu.VMEM((ny // LANES, cz * cx, LANES), f32),
            pltpu.VMEM((2, STEPS, slots, LANES), f32),
            pltpu.VMEM((STEPS, 2, 2, cz, ny), f32),
            pltpu.VMEM((STEPS, 2, 2, cz, ny), f32),
            pltpu.VMEM((STEPS, 2, 2, cx, ny), f32),
            pltpu.SemaphoreType.DMA((STEPS, 2, 4)),
            pltpu.SemaphoreType.DMA((STEPS, 2, 4)),
        ],
        compiler_params=pltpu.CompilerParams(
            collective_id=0, has_side_effects=True, vmem_limit_bytes=50 * 1024 * 1024
        ),
    )(p_now, p_prev, a_now, a_prev, speed2, src.reshape(1, slots), src.reshape(slots, 1), relay)


def body(
    nx, nz, pressure_now, pressure_prev, adjoint_now, adjoint_prev, speed2,
    layer_state, layer_maps, send_rows, slot_patch, patch_material,
):
    slots, _, width = layer_state.shape
    devices = nx * nz
    patches = patch_material.shape[0]
    cap = send_rows.shape[2]
    axes = ("gx", "gz")
    rows = project(slot_patch, patch_material, layer_maps, layer_state)
    relay = lax.all_to_all(
        rows.reshape(ROWS, devices, cap, width), axes, split_axis=1, concat_axis=1, tiled=True
    ).reshape(ROWS, slots, width)
    pressure_out, adjoint_out, corr = wave(
        nx, nz, pressure_now, pressure_prev, adjoint_now, adjoint_prev, speed2,
        send_rows.reshape(-1), relay,
    )
    patch = relay[ROWS - 1, :, ROWS - 1].astype(jnp.int32)
    owners = (patch[:, None] == jnp.arange(patches, dtype=jnp.int32)[None, :]).astype(jnp.float32)
    local = jnp.einsum("sp,sw->pw", owners, corr, precision=lax.Precision.HIGHEST)
    parts = lax.all_to_all(
        local.reshape(devices, patches // devices, width), axes, split_axis=0, concat_axis=0, tiled=True
    )
    gradient = jnp.sum(parts, axis=0)
    return pressure_out, adjoint_out, gradient


def solution(mesh):
    in_specs = (
        P("gz", "gx", None),
        P("gz", "gx", None),
        P("gz", "gx", None),
        P("gz", "gx", None),
        P("gz", "gx", None),
        P(("gx", "gz"), None, None),
        P(),
        P(("gx", "gz"), None, None),
        P(("gx", "gz")),
        P(),
    )
    out_specs = (P("gz", "gx", None), P("gz", "gx", None), P(("gx", "gz"), None))
    return jax.shard_map(
        functools.partial(body, mesh.shape["gx"], mesh.shape["gz"]),
        mesh=mesh, in_specs=in_specs, out_specs=out_specs, check_vma=False,
    )
```

```python
import functools

import jax
import jax.numpy as jnp
from jax import lax
from jax.experimental import pallas as pl
from jax.experimental.pallas import tpu as pltpu
from jax.sharding import PartitionSpec as P

STEPS = 4
KAPPA = 0.5
BETA = 0.3
ROWS = 2 * STEPS + 1
LANES = 128


def project_kernel(block, slot_patch, patch_material, maps, state, out, table, info):
    mats, depth, _ = maps.shape
    lane = lax.broadcasted_iota(jnp.int32, (1, depth), 1)
    halve = jnp.where(lane == 0, 1.0 - KAPPA, 1.0)
    row8 = lax.broadcasted_iota(jnp.int32, (8, LANES), 0)
    lane8 = lax.broadcasted_iota(jnp.int32, (8, LANES), 1)

    @pl.when(pl.program_id(0) == 0)
    def _():
        v = [maps[m, 0:1, :] for m in range(mats)]
        h = [jnp.zeros_like(v[0])] * mats
        surface, inner = [[] for _ in v], [[] for _ in v]
        for n in range(STEPS):
            for m in range(mats):
                dv = v[m] * halve
                surface[m].append(dv)
                pair = jnp.concatenate([dv, v[m] + h[m]] + [jnp.zeros_like(dv)] * 6, axis=0)
                got = jnp.dot(
                    pair, maps[m], precision=lax.Precision.HIGHEST,
                    preferred_element_type=jnp.float32,
                )
                v[m] = got[0:1]
                h[m] = got[1:2] * halve
                inner[m].append(h[m])
        for m in range(mats):
            rows = jnp.concatenate(surface[m] + inner[m], axis=0)
            high = rows.astype(jnp.bfloat16)
            low = (rows - high.astype(jnp.float32)).astype(jnp.bfloat16)
            table[m] = jnp.concatenate(
                [
                    jnp.concatenate([high, high], axis=1),
                    jnp.concatenate([low, jnp.zeros_like(low)], axis=1),
                ],
                axis=0,
            )
            first = rows[:, 0:1] / (1.0 - KAPPA)
            info[m] = jnp.sum(jnp.where(row8 == lane8, first, 0.0), axis=0, keepdims=True)

    base = pl.program_id(0) * block
    lane1 = lax.broadcasted_iota(jnp.int32, (1, LANES), 1)

    for i in range(block):
        patch = slot_patch[base + i]
        mat = patch_material[patch]
        start = state[i]
        high = start.astype(jnp.bfloat16)
        low = (start - high.astype(jnp.float32)).astype(jnp.bfloat16)
        both = jnp.dot(
            table[mat], jnp.concatenate([high, low], axis=0), preferred_element_type=jnp.float32
        )
        got = both[: 2 * STEPS] + both[2 * STEPS :]
        for n in range(2 * STEPS):
            out[n, i : i + 1, :] = got[n : n + 1]
        patches = jnp.full((1, LANES), patch, jnp.int32).astype(jnp.float32)
        out[2 * STEPS, i : i + 1, :] = jnp.where(lane1 == ROWS - 1, patches, info[mat])


def project(slot_patch, patch_material, maps, state):
    slots, depth, width = state.shape
    mats = maps.shape[0]
    block = 16
    return pl.pallas_call(
        functools.partial(project_kernel, block),
        out_shape=jax.ShapeDtypeStruct((ROWS, slots, width), jnp.float32),
        grid_spec=pltpu.PrefetchScalarGridSpec(
            num_scalar_prefetch=2,
            grid=(slots // block,),
            in_specs=[
                pl.BlockSpec((mats, depth, depth), lambda i, *_: (0, 0, 0)),
                pl.BlockSpec((block, depth, width), lambda i, *_: (i, 0, 0)),
            ],
            out_specs=pl.BlockSpec((ROWS, block, width), lambda i, *_: (0, i, 0)),
            scratch_shapes=[
                pltpu.VMEM((mats, 4 * STEPS, 2 * depth), jnp.bfloat16),
                pltpu.VMEM((mats, 1, width), jnp.float32),
            ],
        ),
    )(slot_patch, patch_material, maps, state)


def wave_kernel(
    nx, nz,
    p_now, p_prev, a_now, a_prev, speed2, src_lane, src_column, relay,
    p_out, a_out, corr,
    p_mid, a_mid, spread, pick, couple, hist,
    x_send, x_recv, z_recv, send_sem, recv_sem,
):
    cz, cx, ny = speed2.shape
    slots = relay.shape[1]
    blocks = ny // LANES
    gx, gz = lax.axis_index("gx"), lax.axis_index("gz")
    exists = [gx > 0, gx < nx - 1, gz > 0, gz < nz - 1]
    target = [(gx - 1, gz), (gx + 1, gz), (gx, gz - 1), (gx, gz + 1)]

    barrier = pltpu.get_barrier_semaphore()
    for d in range(4):
        @pl.when(exists[d])
        def _(d=d):
            pl.semaphore_signal(
                barrier, inc=1, device_id=target[d], device_id_type=pl.DeviceIdType.MESH
            )
    pl.semaphore_wait(barrier, sum(peer.astype(jnp.int32) for peer in exists))

    now = (p_now, a_now)
    prev = (p_prev, a_prev)
    mid = (p_mid, a_mid)
    outs = (p_out, a_out)

    def halo_copy(field, step, d, source):
        if d < 2:
            ref, dst = x_send.at[step, field, d], x_recv.at[step, field, 1 - d]
        else:
            ref = source.at[0 if d == 2 else cz - 1]
            dst = z_recv.at[step, field, 3 - d]
        return pltpu.make_async_remote_copy(
            src_ref=ref, dst_ref=dst,
            send_sem=send_sem.at[step, field, d],
            recv_sem=recv_sem.at[step, field, d ^ 1],
            device_id=target[d], device_id_type=pl.DeviceIdType.MESH,
        )

    def start_halo(field, step, source):
        for d in range(4):
            @pl.when(exists[d])
            def _(d=d):
                halo_copy(field, step, d, source).start()

    def wait_recv(field, step, source):
        for d in range(4):
            @pl.when(exists[d])
            def _(d=d):
                side = x_recv.at[step, field, d] if d < 2 else z_recv.at[step, field, d - 2]
                pltpu.make_async_remote_copy(
                    src_ref=side, dst_ref=side,
                    send_sem=send_sem.at[step, field, d],
                    recv_sem=recv_sem.at[step, field, d],
                    device_id=target[d], device_id_type=pl.DeviceIdType.MESH,
                ).wait_recv()

    def wait_send(field, step, source):
        for d in range(4):
            @pl.when(exists[d])
            def _(d=d):
                halo_copy(field, step, d, source).wait_send()

    for field in range(2):
        @pl.loop(0, cz)
        def _(z, field=field):
            x_send[0, field, 0, pl.ds(z, 1), :] = now[field][z, 0:1, :]
            x_send[0, field, 1, pl.ds(z, 1), :] = now[field][z, cx - 1 : cx, :]
        start_halo(field, 0, now[field])

    for d in range(4):
        @pl.when(jnp.logical_not(exists[d]))
        def _(d=d):
            for step in range(STEPS):
                for field in range(2):
                    if d < 2:
                        x_recv[step, field, d] = jnp.zeros((cz, ny), jnp.float32)
                    else:
                        z_recv[step, field, d - 2] = jnp.zeros((cx, ny), jnp.float32)

    lanes = src_lane[...]
    xrow = lax.broadcasted_iota(jnp.int32, (cx, slots), 0)

    @pl.loop(0, cz)
    def _(z):
        for rb in range(blocks):
            row = z * (cx * blocks) + xrow * blocks + rb
            hit = jnp.where(row == lanes, 1.0, 0.0).astype(jnp.bfloat16)
            spread[rb, pl.ds(pl.multiple_of(z * cx, cx), cx), :] = jnp.concatenate([hit, hit], axis=1)

    lane_row = lax.broadcasted_iota(jnp.int32, (slots, cz * cx), 1) * blocks
    column = src_column[...]
    for rb in range(blocks):
        pick[rb] = jnp.where(lane_row + rb == column, 1.0, 0.0).astype(jnp.bfloat16)

    def gather(source, field, step):
        picked = jnp.zeros((slots, LANES), jnp.float32)
        for rb in range(blocks):
            value = source[:, :, rb * LANES : (rb + 1) * LANES].reshape(cz * cx, LANES)
            high = value.astype(jnp.bfloat16)
            low = (value - high.astype(jnp.float32)).astype(jnp.bfloat16)
            for part in (high, low):
                picked = picked + jnp.dot(pick[rb], part, preferred_element_type=jnp.float32)
        hist[field, step] = picked

    def coef(n):
        return relay[ROWS - 1, :, n : n + 1]

    row_id = lax.broadcasted_iota(jnp.int32, (cx, ny), 0)
    lane_id = lax.broadcasted_iota(jnp.int32, (cx, ny), 1)

    for step in range(STEPS):
        for field in range(2):
            current = (now, mid, outs, mid)[step][field]
            earlier = (prev, now, mid, outs)[step][field]
            result = (mid, outs, mid, outs)[step][field]
            last = step == STEPS - 1

            gather(current, field, step)
            back = relay[step] if field == 0 else jnp.zeros((slots, LANES), jnp.float32)
            for t in range(step + 1):
                back = back + KAPPA * coef(step - t) * hist[field, t]
            delta = BETA * (back - hist[field, step])
            high = delta.astype(jnp.bfloat16)
            low = (delta - high.astype(jnp.float32)).astype(jnp.bfloat16)
            both = jnp.concatenate([high, low], axis=0)

            @pl.loop(0, blocks)
            def _(rb):
                couple[rb] = jnp.dot(spread[rb], both, preferred_element_type=jnp.float32)

            wait_recv(field, step, current)
            if step > 0:
                wait_send(field, step - 1, earlier)

            def plane(z, down, up):
                f = current[z]
                at = pl.multiple_of(z * cx, cx) if not isinstance(z, int) else z * cx
                lo = x_recv[step, field, 0, pl.ds(z, 1), :]
                hi = x_recv[step, field, 1, pl.ds(z, 1), :]
                west = jnp.where(row_id == 0, lo, pltpu.roll(f, 1, 0))
                east = jnp.where(row_id == cx - 1, hi, pltpu.roll(f, cx - 1, 0))
                south = jnp.where(lane_id == 0, 0.0, pltpu.roll(f, 1, 1))
                north = jnp.where(lane_id == ny - 1, 0.0, pltpu.roll(f, ny - 1, 1))
                beside = (down + up) + (west + east) + (south + north)
                extra = jnp.concatenate([couple[rb, pl.ds(at, cx), :] for rb in range(blocks)], axis=1)
                new = 2.0 * f - earlier[z] + speed2[z] * (beside - 6.0 * f) + extra
                result[z] = new
                if not last:
                    x_send[step + 1, field, 0, pl.ds(z, 1), :] = new[0:1]
                    x_send[step + 1, field, 1, pl.ds(z, 1), :] = new[cx - 1 : cx]

            plane(0, z_recv[step, field, 0], current[1])
            plane(cz - 1, current[cz - 2], z_recv[step, field, 1])

            @pl.loop(1, cz - 1, unroll=2)
            def _(z):
                plane(z, current[z - 1], current[z + 1])

            if last:
                wait_send(field, step, current)
            else:
                start_halo(field, step + 1, result)

    total = jnp.zeros((slots, LANES), jnp.float32)
    for t in range(STEPS):
        inner = relay[2 * STEPS - 1 - t]
        for other in range(STEPS - t):
            inner = inner + KAPPA * coef(STEPS + STEPS - 1 - t - other) * hist[0, other]
        total = total + KAPPA * hist[1, t] * inner
    corr[...] = total


def wave(nx, nz, p_now, p_prev, a_now, a_prev, speed2, src, relay):
    cz, cx, ny = speed2.shape
    slots = relay.shape[1]
    f32 = jnp.float32
    vmem = pl.BlockSpec(memory_space=pltpu.VMEM)
    return pl.pallas_call(
        functools.partial(wave_kernel, nx, nz),
        out_shape=(
            jax.ShapeDtypeStruct((cz, cx, ny), f32),
            jax.ShapeDtypeStruct((cz, cx, ny), f32),
            jax.ShapeDtypeStruct((slots, LANES), f32),
        ),
        in_specs=[vmem] * 8,
        out_specs=(vmem, vmem, vmem),
        scratch_shapes=[
            pltpu.VMEM((cz, cx, ny), f32),
            pltpu.VMEM((cz, cx, ny), f32),
            pltpu.VMEM((ny // LANES, cz * cx, 2 * slots), jnp.bfloat16),
            pltpu.VMEM((ny // LANES, slots, cz * cx), jnp.bfloat16),
            pltpu.VMEM((ny // LANES, cz * cx, LANES), f32),
            pltpu.VMEM((2, STEPS, slots, LANES), f32),
            pltpu.VMEM((STEPS, 2, 2, cz, ny), f32),
            pltpu.VMEM((STEPS, 2, 2, cz, ny), f32),
            pltpu.VMEM((STEPS, 2, 2, cx, ny), f32),
            pltpu.SemaphoreType.DMA((STEPS, 2, 4)),
            pltpu.SemaphoreType.DMA((STEPS, 2, 4)),
        ],
        compiler_params=pltpu.CompilerParams(
            collective_id=0, has_side_effects=True, vmem_limit_bytes=50 * 1024 * 1024
        ),
    )(p_now, p_prev, a_now, a_prev, speed2, src.reshape(1, slots), src.reshape(slots, 1), relay)


def body(
    nx, nz, pressure_now, pressure_prev, adjoint_now, adjoint_prev, speed2,
    layer_state, layer_maps, send_rows, slot_patch, patch_material,
):
    slots, _, width = layer_state.shape
    devices = nx * nz
    patches = patch_material.shape[0]
    cap = send_rows.shape[2]
    axes = ("gx", "gz")
    rows = project(slot_patch, patch_material, layer_maps, layer_state)
    relay = lax.all_to_all(
        rows.reshape(ROWS, devices, cap, width), axes, split_axis=1, concat_axis=1, tiled=True
    ).reshape(ROWS, slots, width)
    pressure_out, adjoint_out, corr = wave(
        nx, nz, pressure_now, pressure_prev, adjoint_now, adjoint_prev, speed2,
        send_rows.reshape(-1), relay,
    )
    patch = relay[ROWS - 1, :, ROWS - 1].astype(jnp.int32)
    owners = (patch[:, None] == jnp.arange(patches, dtype=jnp.int32)[None, :]).astype(jnp.float32)
    local = jnp.einsum("sp,sw->pw", owners, corr, precision=lax.Precision.HIGHEST)
    parts = lax.all_to_all(
        local.reshape(devices, patches // devices, width), axes, split_axis=0, concat_axis=0, tiled=True
    )
    gradient = jnp.sum(parts, axis=0)
    return pressure_out, adjoint_out, gradient


def solution(mesh):
    in_specs = (
        P("gz", "gx", None),
        P("gz", "gx", None),
        P("gz", "gx", None),
        P("gz", "gx", None),
        P("gz", "gx", None),
        P(("gx", "gz"), None, None),
        P(),
        P(("gx", "gz"), None, None),
        P(("gx", "gz")),
        P(),
    )
    out_specs = (P("gz", "gx", None), P("gz", "gx", None), P(("gx", "gz"), None))
    return jax.shard_map(
        functools.partial(body, mesh.shape["gx"], mesh.shape["gz"]),
        mesh=mesh, in_specs=in_specs, out_specs=out_specs, check_vma=False,
    )
```
